32 devices in a mesh: groups: 2 (over y), tensor: 4 (over z), store: 4 (over x, core).
Axes of the slice: x: 2, y: 2, z: 4, core: 2. Of those that a mesh axis runs over, the one named last changes fastest.
Arguments:
- tokens: bfloat16 [4096, 8192], P(('groups', 'store', 'tensor')), parts along dimension 0, may hold values from -32 to 32
- query_weight: bfloat16 [8192, 8192], P(None, 'tensor'), may hold values from -0.0625 to 0.0625
- key_value_weight: bfloat16 [8192, 2048], P(None, 'tensor'), may hold values from -0.0625 to 0.0625
- adapter_down_maps: bfloat16 [32, 128, 8192], P('store', None, 'tensor'), may hold values from -0.0625 to 0.0625
- adapter_up_query: bfloat16 [32, 64, 8192], P('store', None, 'tensor'), may hold values from -0.375 to 0.375
- adapter_up_key_value: bfloat16 [32, 64, 2048], P('store', None, 'tensor'), may hold values from -0.375 to 0.375
- adapter_row_table: int32 [64], P('groups'), parts along dimension 0, may hold values from 0 to 31, as said below
- request_adapter_ids: int32 [8, 4], P('groups'), parts along dimension 0, may hold values from 0 to 31, as said below
- token_request_ids: int32 [8, 512], P(('groups', 'store')), parts along dimension 0, may hold values from 0 to 3, never falling along the last dimension, each value on 1 to 256 neighbouring positions
Outputs:
- attention: bfloat16 [4096, 8192], P(('groups', 'store'), 'tensor'), parts along dimension 0
The draws below stay inside these ranges and needn't reach their ends.
There are 2 independent parts, one for each index of `groups`. The reference program is written for one: setup_inputs(seed, part) draws one part's arguments, and reference() takes and returns one part's arrays. A program takes and returns all parts, laid end to end along the dimension named above; an argument that names none is the same for every part. Nothing has to cross between parts.
Inputs may be any that keep to these rules, and one draw needn't show every extreme that they name: A permutation: adapter a lies in row adapter_row_table[a] of the adapter arrays, on store index adapter_row_table[a] // 8. `request_adapter_ids`: the 4 requests of one store batch use adapters held on 4 different store indices. `token_request_ids`: requests are contiguous runs of a store batch, each of 1 to 256 tokens.
All inputs are finite; a program needn't handle non-finite values.
Results may differ from the reference program's by a relative error of at most 0.012.
The reference program's roundings to bfloat16 on the way (of `low`, `query`, `keys`, `values` and `weights`) count: a program that leaves them out, or rounds other values in their place, can miss the bound.
Values may be sent and summed in bfloat16 or wider, within the bound.
A program may use at most 128 MiB of HBM per device.

```python
import math
import jax
import jax.numpy as jnp
import numpy as np
from jax import lax

MODEL_WIDTH = 8192
QUERY_HEADS = 64
KEY_VALUE_HEADS = 8
HEAD_SIZE = 128
ADAPTER_RANK = 64
STORE_REQUESTS = 4
TOK_ST = 512
SLOTS = 8
TOKENS = 2048
ADAPTER_COUNT = 32
N_TENSOR = 4
N_STORE = 4


def draw_tokens(key, part):
    values = jnp.clip(jax.random.normal(jax.random.fold_in(key, 3), (TOKENS, MODEL_WIDTH), jnp.float32), -4.0, 4.0)
    return values.astype(jnp.bfloat16)


def place_slot(owners, locals_table, row_pick, col_pick, slot_value):
    target = slot_value // SLOTS
    row_index = jnp.arange(N_STORE, dtype=jnp.int32)[:, None]
    col_index = jnp.arange(N_STORE, dtype=jnp.int32)[None, :]
    in_row = row_index == row_pick
    current = owners[row_pick, col_pick]
    moved = jnp.where(in_row & (owners == target), current, owners)
    moved = jnp.where(in_row & (col_index == col_pick), target, moved)
    locals_new = jnp.where(in_row & (col_index == col_pick), slot_value % SLOTS, locals_table)
    return (moved, locals_new)


def owner_rows(row_key):
    return jax.random.permutation(row_key, N_STORE).astype(jnp.int32)


def placement_tables(key):
    adapter_total = SLOTS * N_STORE
    order = jax.random.permutation(jax.random.fold_in(key, 21), adapter_total).astype(jnp.int32)
    inverse = jnp.zeros((adapter_total,), jnp.int32).at[order].set(jnp.arange(adapter_total, dtype=jnp.int32))
    row_keys = jax.random.split(jax.random.fold_in(key, 22), N_STORE)
    owners = jax.vmap(owner_rows)(row_keys)
    locals_table = jax.random.randint(jax.random.fold_in(key, 23), (N_STORE, N_STORE), 0, SLOTS).astype(jnp.int32)
    first_row = jax.random.randint(jax.random.fold_in(key, 24), (), 0, N_STORE).astype(jnp.int32)
    second_row = ((first_row + 1 + jax.random.randint(jax.random.fold_in(key, 25), (), 0, N_STORE - 1)) % N_STORE).astype(jnp.int32)
    first_col = jax.random.randint(jax.random.fold_in(key, 26), (), 0, STORE_REQUESTS).astype(jnp.int32)
    second_col = jax.random.randint(jax.random.fold_in(key, 27), (), 0, STORE_REQUESTS).astype(jnp.int32)
    owners, locals_table = place_slot(owners, locals_table, first_row, first_col, order[adapter_total - 1])
    owners, locals_table = place_slot(owners, locals_table, second_row, second_col, order[0])
    positions_list = owners[:, :STORE_REQUESTS] * SLOTS + locals_table[:, :STORE_REQUESTS]
    return (order, inverse[positions_list].astype(jnp.int32))


def draw_adapter_row_table(key, part):
    return placement_tables(key)[0]


def draw_request_adapter_ids(key, part):
    return placement_tables(key)[1]


def steps_of(own_key, shape, shards, smallest, top_value):
    def one(axis_at, shards_of):
        draws = jax.random.uniform(jax.random.fold_in(jax.random.fold_in(own_key, 6), axis_at), (shards_of,), jnp.float32, smallest / len(shards), top_value / len(shards))
        return jnp.repeat(jnp.exp(draws), shape[axis_at] // shards_of).reshape((-1,) + (1,) * (len(shape) - axis_at - 1))

    loudness = one(*shards[0])
    for cut in shards[1:]:
        loudness = loudness * one(*cut)
    return loudness


def length_profile(count, total, limit, skew):
    weights = [(1 << 20) // math.isqrt(standing ** skew) + 1 for standing in range(2, count + 1)]
    surplus, holding = total - limit - (count - 1), [1] * (count - 1)
    while surplus > 0:
        candidates = [i for i in range(count - 1) if holding[i] < limit]
        mass, remaining = sum([weights[i] for i in candidates]), surplus
        for i in candidates:
            extra = min(limit - holding[i], max(1, remaining * weights[i] // mass), surplus)
            holding[i] = holding[i] + extra
            surplus = surplus - extra
    return np.array([limit] + holding)


def uneven_parts(rng, amount, total, bound, skew):
    if amount == 2:
        one = jax.random.randint(rng, (), max(1, total - bound), min(bound, total - 1) + 1)
        return jnp.stack([one, total - one])
    tallies = jnp.asarray(length_profile(amount, total, bound, skew), jnp.int32)
    couples = (amount - 1) // 2
    giver, taker = tallies[1:1 + 2 * couples:2], tallies[2:2 + 2 * couples:2]
    slack = jnp.minimum(giver - 1, bound - taker)
    passed = jax.random.randint(jax.random.fold_in(rng, 1), (couples,), 0, 1 << 20) % (slack + 1)
    tallies = tallies.at[1:1 + 2 * couples:2].set(giver - passed).at[2:2 + 2 * couples:2].set(taker + passed)
    return tallies[jax.random.permutation(jax.random.fold_in(rng, 2), amount)]


def noise(rng, shape, scale, bound, pieces=(), held_as=jnp.bfloat16):
    values = scale * jax.random.normal(rng, shape, jnp.float32)
    if pieces:
        values = values * steps_of(rng, shape, pieces, -0.22, 0.18)
    return jnp.clip(values, -bound, bound).astype(held_as)


def setup_inputs(seed: int = 0, part: int = 0) -> dict:
    seeds = jax.random.split(jax.random.key(seed), 10)
    part_splits = jax.random.split(jax.random.fold_in(seeds[9], part), 10)
    return {
        "tokens": draw_tokens(jax.random.fold_in(jax.random.fold_in(seeds[9], part), 71), part),
        "query_weight": noise(seeds[1], (MODEL_WIDTH, QUERY_HEADS * HEAD_SIZE), MODEL_WIDTH ** -0.5, 0.0625, ((1, 4),)),
        "key_value_weight": noise(seeds[2], (MODEL_WIDTH, 2 * KEY_VALUE_HEADS * HEAD_SIZE), MODEL_WIDTH ** -0.5, 0.0625, ((1, 4),)),
        "adapter_down_maps": noise(seeds[3], (ADAPTER_COUNT, 2 * ADAPTER_RANK, MODEL_WIDTH), MODEL_WIDTH ** -0.5, 0.0625, ((0, 4), (2, 4))),
        "adapter_up_query": noise(seeds[4], (ADAPTER_COUNT, ADAPTER_RANK, QUERY_HEADS * HEAD_SIZE), (4 * ADAPTER_RANK) ** -0.5, 0.375, ((0, 4), (2, 4))),
        "adapter_up_key_value": noise(seeds[5], (ADAPTER_COUNT, ADAPTER_RANK, 2 * KEY_VALUE_HEADS * HEAD_SIZE), (4 * ADAPTER_RANK) ** -0.5, 0.375, ((0, 4), (2, 4))),
        "adapter_row_table": draw_adapter_row_table(jax.random.fold_in(jax.random.fold_in(seeds[9], part), 71), part),
        "request_adapter_ids": draw_request_adapter_ids(jax.random.fold_in(jax.random.fold_in(seeds[9], part), 71), part),
        "token_request_ids": jax.vmap(lambda own: jnp.searchsorted(jnp.cumsum(uneven_parts(own, STORE_REQUESTS, TOK_ST, TOK_ST // 2, 2)), jnp.arange(TOK_ST), side="right"))(jax.random.split(part_splits[8], N_STORE)).reshape((N_STORE, TOK_ST)).astype(jnp.int32),
    }


adapter_scale = 2.0
rope_theta = 500000.0

def token_positions(segment_row):
    members = segment_row[:, None] == jnp.arange(STORE_REQUESTS, dtype=jnp.int32)[None, :]
    counts = lax.optimization_barrier(jnp.sum(members.astype(jnp.int32), axis=0)).astype(jnp.int32)
    starts = (jnp.cumsum(counts) - counts).astype(jnp.int32)
    first_index = lax.optimization_barrier(jnp.sum(jnp.where(members, starts[None, :], 0), axis=1)).astype(jnp.int32)
    return jnp.arange(segment_row.shape[0], dtype=jnp.int32) - first_index

def rotary(heads_values, positions):
    half_size = heads_values.shape[-1] // 2
    exponent = jnp.arange(half_size, dtype=jnp.float32) * (2.0 / heads_values.shape[-1])
    frequency = jnp.exp(-exponent * math.log(rope_theta))
    angles = positions.astype(jnp.float32)[:, None] * frequency[None, :]
    cosine = jnp.cos(angles)[:, None, :]
    sine = jnp.sin(angles)[:, None, :]
    lower = heads_values[..., :half_size]
    upper = heads_values[..., half_size:]
    return jnp.concatenate([lower * cosine - upper * sine, upper * cosine + lower * sine], axis=-1)

def reference(tokens, query_weight, key_value_weight, adapter_down_maps, adapter_up_query, adapter_up_key_value, adapter_row_table, request_adapter_ids, token_request_ids):
    group_size = QUERY_HEADS // KEY_VALUE_HEADS
    pair_count = N_TENSOR // 2
    pair_heads = 2 * KEY_VALUE_HEADS // N_TENSOR
    slot_table = adapter_row_table[request_adapter_ids].astype(jnp.int32)
    batches = tokens.reshape(N_STORE, TOK_ST, MODEL_WIDTH)

    def one_batch(inputs):
        gathered_rows, positions_list, segment_row = inputs
        members = segment_row[:, None] == jnp.arange(STORE_REQUESTS, dtype=jnp.int32)[None, :]
        member_float = members.astype(jnp.float32)
        member_half = members.astype(jnp.bfloat16)
        down_product = adapter_down_maps[positions_list].astype(jnp.float32)
        projected = jnp.einsum('td,krd->tkr', gathered_rows.astype(jnp.float32), down_product)
        low = lax.optimization_barrier(jnp.sum(projected * member_float[:, :, None], axis=1)).astype(jnp.bfloat16)
        token_query_update = (low[:, None, :ADAPTER_RANK] * member_half[:, :, None]).reshape(TOK_ST, STORE_REQUESTS * ADAPTER_RANK)
        token_key_value_update = (low[:, None, ADAPTER_RANK:] * member_half[:, :, None]).reshape(TOK_ST, STORE_REQUESTS * ADAPTER_RANK)
        query_update = jnp.dot(token_query_update, adapter_up_query[positions_list].reshape(STORE_REQUESTS * ADAPTER_RANK, QUERY_HEADS * HEAD_SIZE), preferred_element_type=jnp.float32)
        key_value_update = jnp.dot(token_key_value_update, adapter_up_key_value[positions_list].reshape(STORE_REQUESTS * ADAPTER_RANK, 2 * KEY_VALUE_HEADS * HEAD_SIZE), preferred_element_type=jnp.float32)
        query_unrotated = jnp.dot(gathered_rows, query_weight, preferred_element_type=jnp.float32) + adapter_scale * query_update
        key_value_unrotated = jnp.dot(gathered_rows, key_value_weight, preferred_element_type=jnp.float32) + adapter_scale * key_value_update
        positions = token_positions(segment_row)
        query = rotary(query_unrotated.reshape(TOK_ST, QUERY_HEADS, HEAD_SIZE), positions).astype(jnp.bfloat16)
        keyval = key_value_unrotated.reshape(TOK_ST, pair_count, 2, pair_heads, HEAD_SIZE)
        keys = rotary(keyval[:, :, 0].reshape(TOK_ST, KEY_VALUE_HEADS, HEAD_SIZE), positions).astype(jnp.bfloat16)
        values = keyval[:, :, 1].reshape(TOK_ST, KEY_VALUE_HEADS, HEAD_SIZE).astype(jnp.bfloat16)
        grouped = query.reshape(TOK_ST, KEY_VALUE_HEADS, group_size, HEAD_SIZE)
        scores = jnp.einsum('tkgd,skd->kgts', grouped.astype(jnp.float32), keys.astype(jnp.float32)) / math.sqrt(HEAD_SIZE)
        token_index = jnp.arange(TOK_ST, dtype=jnp.int32)
        allowed = (segment_row[:, None] == segment_row[None, :]) & (token_index[:, None] >= token_index[None, :])
        scores = jnp.where(allowed, scores, -1e+30)
        scores = scores - lax.optimization_barrier(jnp.max(scores, axis=-1, keepdims=True))
        weights = jnp.exp(scores)
        weights = (weights / lax.optimization_barrier(jnp.sum(weights, axis=-1, keepdims=True))).astype(jnp.bfloat16)
        mixed = jnp.einsum('kgts,skd->tkgd', weights.astype(jnp.float32), values.astype(jnp.float32))
        return mixed.reshape(TOK_ST, QUERY_HEADS * HEAD_SIZE).astype(jnp.bfloat16)
    result = lax.map(one_batch, (batches, slot_table, token_request_ids))
    return result.reshape(TOKENS, QUERY_HEADS * HEAD_SIZE)
```

```python
import functools
import math

import jax
import jax.numpy as jnp
from jax import lax
from jax.experimental import pallas as pl
from jax.experimental.pallas import tpu as pltpu
from jax.sharding import PartitionSpec as P

MODEL_WIDTH = 8192
QUERY_HEADS = 64
KEY_VALUE_HEADS = 8
HEAD_SIZE = 128
ADAPTER_RANK = 64
STORE_REQUESTS = 4
TOK_ST = 512


adapter_scale = 2.0
rope_theta = 500000.0


def token_positions(segment_row):
    members = segment_row[:, None] == jnp.arange(STORE_REQUESTS, dtype=jnp.int32)[None, :]
    counts = jnp.sum(members.astype(jnp.int32), axis=0)
    starts = jnp.cumsum(counts) - counts
    first_index = jnp.sum(jnp.where(members, starts[None, :], 0), axis=1)
    return jnp.arange(segment_row.shape[0], dtype=jnp.int32) - first_index


MAX_RUN = 256
MESH = pl.DeviceIdType.MESH


def rotary_tables(positions):
    half_size = HEAD_SIZE // 2
    exponent = jnp.arange(half_size, dtype=jnp.float32) * (2.0 / HEAD_SIZE)
    frequency = jnp.exp(-exponent * math.log(rope_theta))
    angles = positions.astype(jnp.float32)[:, None] * frequency[None, :]
    cosine = jnp.cos(angles)
    sine = jnp.sin(angles)
    return (
        jnp.concatenate([cosine, cosine], axis=1),
        jnp.concatenate([-sine, sine], axis=1),
    )


def select_kernel(index_ref, down_ref, query_ref, keyval_ref, down_out, query_out, keyval_out):
    down_out[...] = down_ref[...]
    query_out[...] = query_ref[...]
    keyval_out[...] = keyval_ref[...]


def select_adapters(index, stacks):
    specs_in = [
        pl.BlockSpec((1,) + stack.shape[1:], lambda i, index_ref: (index_ref[i], 0, 0))
        for stack in stacks
    ]
    specs_out = [
        pl.BlockSpec((1,) + stack.shape[1:], lambda i, index_ref: (i, 0, 0)) for stack in stacks
    ]
    return pl.pallas_call(
        select_kernel,
        grid_spec=pltpu.PrefetchScalarGridSpec(
            num_scalar_prefetch=1,
            grid=(index.shape[0],),
            in_specs=specs_in,
            out_specs=specs_out,
        ),
        out_shape=[
            jax.ShapeDtypeStruct((index.shape[0],) + stack.shape[1:], stack.dtype)
            for stack in stacks
        ],
        name="select_adapters",
    )(index, *stacks)


def project_kernel(
    n,
    stores,
    chunks,
    tokens_ref,
    wq_hbm,
    wkv_hbm,
    down_hbm,
    upq_hbm,
    upkv_hbm,
    mask_ref,
    cos_ref,
    sin_ref,
    kcos_ref,
    ksin_ref,
    query_out,
    own_out,
    other_out,
    xbuf,
    wq,
    wkv,
    acc_q,
    acc_kv,
    down,
    upq,
    upkv,
    low_part,
    low_got,
    low_all,
    kv_heads,
    kv_got,
    token_sem,
    weight_sem,
    recv_sem,
    send_sem,
    adapter_send,
    adapter_recv,
    adapter_own,
    part_send,
    part_recv,
    low_send,
    low_recv,
    kv_sem,
):
    t = lax.axis_index("tensor")
    s = lax.axis_index("store")
    rows = tokens_ref.shape[0]
    width = tokens_ref.shape[1] // chunks
    total = rows * n
    query_width = wq.shape[1]
    keyval_width = wkv.shape[1]
    pair_heads = keyval_width // HEAD_SIZE
    head_local = query_width // HEAD_SIZE
    group_size = QUERY_HEADS // KEY_VALUE_HEADS
    kv_used = max(head_local // group_size, 1)

    def kv_first(rank):
        return rank * head_local // group_size - rank // 2 * pair_heads

    barrier = pltpu.get_barrier_semaphore()
    for d in range(1, n):
        pl.semaphore_signal(
            barrier, inc=1, device_id={"tensor": lax.rem(t + d, n)}, device_id_type=MESH
        )
    for d in range(1, stores):
        pl.semaphore_signal(
            barrier, inc=1, device_id={"store": lax.rem(s + d, stores)}, device_id_type=MESH
        )

    def own_copy(c):
        return pltpu.make_async_copy(
            tokens_ref.at[:, pl.ds(c * width, width)],
            xbuf.at[c, pl.ds(t * rows, rows), :],
            token_sem.at[c],
        )

    def weight_copies(c):
        part = pl.ds(c * width, width)
        return (
            pltpu.make_async_copy(wq_hbm.at[part, :], wq.at[part, :], weight_sem.at[0, c]),
            pltpu.make_async_copy(wkv_hbm.at[part, :], wkv.at[part, :], weight_sem.at[1, c]),
        )

    for c in range(chunks):
        own_copy(c).start()
        for copy in weight_copies(c):
            copy.start()
    adapter_pairs = ((down_hbm, down), (upq_hbm, upq), (upkv_hbm, upkv))

    def adapter_block(held, i, at):
        if i == 0:
            return held.at[at]
        return held.at[pl.ds(at * ADAPTER_RANK, ADAPTER_RANK), :]

    own_adapters = [
        pltpu.make_async_copy(source.at[s], adapter_block(held, i, s), adapter_own.at[i])
        for i, (source, held) in enumerate(adapter_pairs)
    ]
    for copy in own_adapters:
        copy.start()

    pl.semaphore_wait(barrier, n - 1 + stores - 1)

    def place(side, i):
        return chunks - 1 - i if side == 0 else i

    def stream_copy(side, p, i, own):
        c = place(side, i)
        shard = t - p if side == 0 else t + p
        held = xbuf.at[c, pl.ds(shard * rows, rows), :]
        source = tokens_ref.at[:, pl.ds(c * width, width)] if own else held
        return pltpu.make_async_remote_copy(
            src_ref=source,
            dst_ref=held,
            send_sem=send_sem.at[side, p, i],
            recv_sem=recv_sem.at[side, p, i],
            device_id={"tensor": t + 1 if side == 0 else t - 1},
            device_id_type=MESH,
        )

    def arrival(side, p, i):
        c = place(side, i)
        shard = t - p if side == 0 else t + p
        held = xbuf.at[c, pl.ds(shard * rows, rows), :]
        return pltpu.make_async_remote_copy(
            src_ref=held,
            dst_ref=held,
            send_sem=send_sem.at[side, p - 1, i],
            recv_sem=recv_sem.at[side, p - 1, i],
            device_id={"tensor": t - 1 if side == 0 else t + 1},
            device_id_type=MESH,
        )

    can_send = (t < n - 1, t > 0)
    for i in range(chunks):
        for side in range(2):

            @pl.when(can_send[side])
            def _():
                stream_copy(side, 0, i, True).start()

    adapter_sends = []
    for d in range(1, stores):
        for i, (source, held) in enumerate(adapter_pairs):
            peer = lax.rem(s + d, stores)
            copy = pltpu.make_async_remote_copy(
                src_ref=source.at[peer],
                dst_ref=adapter_block(held, i, s),
                send_sem=adapter_send.at[i, d],
                recv_sem=adapter_recv.at[i, d],
                device_id={"store": peer},
                device_id_type=MESH,
            )
            copy.start()
            adapter_sends.append(copy)

    tile_q = min(query_width, 512)

    def unit(c, shard, first):
        at = pl.ds(pl.multiple_of(shard * rows, rows), rows)
        part = pl.ds(pl.multiple_of(c * width, width), width)
        x = xbuf[c, at, :]
        add = jnp.dot(x, wkv[part, :], preferred_element_type=jnp.float32)
        if first:
            acc_kv[at, :] = add
        else:
            acc_kv[at, :] += add

        @pl.loop(0, query_width // tile_q)
        def _(k):
            columns = pl.ds(pl.multiple_of(k * tile_q, tile_q), tile_q)
            more = jnp.dot(
                xbuf[c, at, :], wq[part, columns], preferred_element_type=jnp.float32
            )
            if first:
                acc_q[at, columns] = more
            else:
                acc_q[at, columns] += more

    acc_q[...] = jnp.zeros_like(acc_q)
    acc_kv[...] = jnp.zeros_like(acc_kv)

    @pl.loop(0, chunks)
    def _(c):
        own_copy(c).wait()
        for copy in weight_copies(c):
            copy.wait()
        unit(c, t, False)

    for copy in own_adapters:
        copy.wait()

    share = chunks // n
    last_phase = jnp.maximum(t, n - 1 - t)
    low_at = share * (jnp.minimum(t, n - 1 - t) + 1) - 1

    def part_copy(d):
        to = lax.rem(t + d, n)
        return pltpu.make_async_remote_copy(
            src_ref=low_part.at[pl.ds(to * rows, rows), :],
            dst_ref=low_got.at[t],
            send_sem=part_send.at[d],
            recv_sem=part_recv.at[d],
            device_id={"tensor": to},
            device_id_type=MESH,
        )

    def part_arrival(d):
        source = lax.rem(t + n - d, n)
        return pltpu.make_async_remote_copy(
            src_ref=low_got.at[source],
            dst_ref=low_got.at[source],
            send_sem=part_send.at[d],
            recv_sem=part_recv.at[d],
            device_id={"tensor": source},
            device_id_type=MESH,
        )

    def low_copy(d):
        to = lax.rem(t + d, n)
        held = low_all.at[pl.ds(t * rows, rows), :]
        return pltpu.make_async_remote_copy(
            src_ref=held,
            dst_ref=held,
            send_sem=low_send.at[d],
            recv_sem=low_recv.at[d],
            device_id={"tensor": to},
            device_id_type=MESH,
        )

    def low_arrival(d):
        source = lax.rem(t + n - d, n)
        held = low_all.at[pl.ds(source * rows, rows), :]
        return pltpu.make_async_remote_copy(
            src_ref=held,
            dst_ref=held,
            send_sem=low_send.at[d],
            recv_sem=low_recv.at[d],
            device_id={"tensor": source},
            device_id_type=MESH,
        )

    def adapters_arrive():
        for d in range(1, stores):
            source = lax.rem(s + stores - d, stores)
            for i, (_, held) in enumerate(adapter_pairs):
                block = adapter_block(held, i, source)
                pltpu.make_async_remote_copy(
                    src_ref=block,
                    dst_ref=block,
                    send_sem=adapter_send.at[i, d],
                    recv_sem=adapter_recv.at[i, d],
                    device_id={"store": source},
                    device_id_type=MESH,
                ).wait_recv()

    def low_first():
        adapters_arrive()
        low_part[...] = jnp.zeros_like(low_part)
        for p in range(stores):
            picked = jnp.zeros(low_part.shape, jnp.float32)
            for k in range(share):
                picked += lax.dot_general(
                    xbuf[t * share + k],
                    down[p, :, k * width : (k + 1) * width],
                    (((1,), (1,)), ((), ())),
                    preferred_element_type=jnp.float32,
                )
            low_part[...] += picked * mask_ref[:, p : p + 1]
        for d in range(1, n):
            part_copy(d).start()

    def low_second():
        at = pl.ds(pl.multiple_of(t * rows, rows), rows)
        low_got[t] = low_part[at, :]
        for d in range(1, n):
            part_arrival(d).wait_recv()
        whole = low_got[0]
        for j in range(1, n):
            whole += low_got[j]
        low_all[at, :] = whole.astype(jnp.bfloat16)
        for d in range(1, n):
            low_copy(d).start()

    def low_third():
        for d in range(1, n):
            low_arrival(d).wait_recv()
        low = low_all[...].astype(jnp.float32)
        turned = pltpu.roll(low, ADAPTER_RANK, 1)
        in_lower = lax.broadcasted_iota(jnp.int32, low.shape, 1) < ADAPTER_RANK
        twice_q = jnp.where(in_lower, low, turned)
        twice_kv = jnp.where(in_lower, turned, low)
        masks = [
            jnp.where(in_lower, mask_ref[:, 2 * p : 2 * p + 1], mask_ref[:, 2 * p + 1 : 2 * p + 2])
            for p in range(stores // 2)
        ]
        spread_q = jnp.concatenate([(twice_q * m).astype(jnp.bfloat16) for m in masks], axis=1)
        spread_kv = jnp.concatenate([(twice_kv * m).astype(jnp.bfloat16) for m in masks], axis=1)
        acc_kv[...] += adapter_scale * jnp.dot(
            spread_kv, upkv[...], preferred_element_type=jnp.float32
        )
        for k in range(query_width // tile_q):
            columns = slice(k * tile_q, (k + 1) * tile_q)
            acc_q[:, columns] += adapter_scale * jnp.dot(
                spread_q, upq[:, columns], preferred_element_type=jnp.float32
            )

    depth = min(2, chunks)

    @pl.loop(0, (n - 1) * chunks)
    def _(step):
        p = step // chunks + 1
        i = step % chunks
        here = (t - p >= 0, t + p < n)
        for side in range(2):

            @pl.when(jnp.logical_and(here[side], can_send[side]))
            def _():
                back = step + chunks - depth
                arrival(side, p, i).wait_recv()
                stream_copy(side, back // chunks, back % chunks, False).wait_send()
                stream_copy(side, p, i, False).start()

            @pl.when(jnp.logical_and(here[side], jnp.logical_not(can_send[side])))
            def _():
                arrival(side, p, i).wait_recv()

        for side in range(2):

            @pl.when(here[side])
            def _():
                unit(place(side, i), t - p if side == 0 else t + p, False)

        @pl.when(jnp.logical_and(p == last_phase, i == low_at))
        def _():
            low_first()

        @pl.when(jnp.logical_and(p == last_phase, i == low_at + 2))
        def _():
            low_second()

        @pl.when(jnp.logical_and(p == last_phase, i == chunks - 2))
        def _():
            low_third()

    def rotated(value, cosine, sine):
        return value * cosine + pltpu.roll(value, HEAD_SIZE // 2, 1) * sine

    for m in range(pair_heads):
        value = acc_kv[:, m * HEAD_SIZE : (m + 1) * HEAD_SIZE]
        kv_heads[m] = rotated(value, kcos_ref[...], ksin_ref[...]).astype(jnp.bfloat16)
    partner = t + 1 - 2 * (t % 2)
    kv_copy = pltpu.make_async_remote_copy(
        src_ref=kv_heads.at[pl.ds(kv_first(partner), kv_used)],
        dst_ref=kv_got,
        send_sem=kv_sem.at[0],
        recv_sem=kv_sem.at[1],
        device_id={"tensor": partner},
        device_id_type=MESH,
    )
    kv_copy.start()
    for h in range(head_local):
        columns = slice(h * HEAD_SIZE, (h + 1) * HEAD_SIZE)
        query_out[:, columns] = rotated(acc_q[:, columns], cos_ref[...], sin_ref[...]).astype(
            jnp.bfloat16
        )
    own_out[...] = kv_heads[pl.ds(kv_first(t), kv_used)]
    for copy in adapter_sends:
        copy.wait_send()
    for d in range(1, n):
        part_copy(d).wait_send()
        low_copy(d).wait_send()

    @pl.loop(0, chunks - depth)
    def _(k):
        for side in range(2):

            @pl.when(can_send[side])
            def _():
                stream_copy(side, 0, k, False).wait_send()

    @pl.loop(0, depth)
    def _(k):
        for side in range(2):

            @pl.when(can_send[side])
            def _():
                reach = t if side == 0 else n - 1 - t
                back = (reach + 1) * chunks - depth + k
                stream_copy(side, back // chunks, back % chunks, False).wait_send()

    kv_copy.wait()
    other_out[...] = kv_got[...]


def attend_kernel(query_ref, keys_ref, values_ref, row_ref, column_ref, out_ref, bias_ref):
    count = query_ref.shape[0]
    block = 128
    scale = 1.0 / math.sqrt(HEAD_SIZE)

    @pl.when(pl.program_id(0) == 0)
    def _():
        place_row = lax.broadcasted_iota(jnp.int32, (count, count), 0)
        place_column = lax.broadcasted_iota(jnp.int32, (count, count), 1)
        allowed = jnp.logical_and(
            column_ref[...] == row_ref[...], place_row >= place_column
        )
        bias_ref[...] = jnp.where(allowed, 0.0, -1e30)

    for b in range(count // block):
        low = max(0, (b + 1) * block - block - MAX_RUN)
        high = (b + 1) * block
        at = slice(b * block, high)
        scores = lax.dot_general(
            query_ref[at, :],
            keys_ref[0, low:high, :],
            (((1,), (1,)), ((), ())),
            preferred_element_type=jnp.float32,
        )
        scores = scores * scale + bias_ref[at, low:high]
        scores = jnp.exp(scores - jnp.max(scores, axis=1, keepdims=True))
        weights = (scores * (1.0 / jnp.sum(scores, axis=1, keepdims=True))).astype(jnp.bfloat16)
        out_ref[at, :] = jnp.dot(
            weights, values_ref[0, low:high, :], preferred_element_type=jnp.float32
        ).astype(jnp.bfloat16)


def attend(query, keys, values, segment_row):
    count, query_width = query.shape
    head_local = query_width // HEAD_SIZE
    per_kv = head_local // keys.shape[0]
    kv_spec = pl.BlockSpec((1, count, HEAD_SIZE), lambda h: (h // per_kv, 0, 0))
    return pl.pallas_call(
        attend_kernel,
        grid=(head_local,),
        in_specs=[
            pl.BlockSpec((count, HEAD_SIZE), lambda h: (0, h)),
            kv_spec,
            kv_spec,
            pl.BlockSpec((1, count), lambda h: (0, 0)),
            pl.BlockSpec((count, 1), lambda h: (0, 0)),
        ],
        out_specs=pl.BlockSpec((count, HEAD_SIZE), lambda h: (0, h)),
        out_shape=jax.ShapeDtypeStruct((count, query_width), jnp.bfloat16),
        scratch_shapes=[pltpu.VMEM((count, count), jnp.float32)],
        name="attend",
    )(query, keys, values, segment_row[None, :], segment_row[:, None])


def on_device(
    tokens,
    query_weight,
    key_value_weight,
    adapter_down_maps,
    adapter_up_query,
    adapter_up_key_value,
    adapter_row_table,
    request_adapter_ids,
    token_request_ids,
):
    tensor_rank = lax.axis_index("tensor")
    store_rank = lax.axis_index("store")
    n = lax.axis_size("tensor")
    stores = lax.axis_size("store")
    position_count = adapter_down_maps.shape[0]
    adapter_total = adapter_row_table.shape[0]
    lookup = (
        request_adapter_ids[:, :, None] == jnp.arange(adapter_total, dtype=jnp.int32)[None, None, :]
    ).astype(jnp.int32)
    slot_table = jnp.sum(lookup * adapter_row_table[None, None, :], axis=2)
    my_slots = lax.dynamic_index_in_dim(slot_table, store_rank, 0, keepdims=False)
    mine = slot_table // position_count == store_rank
    index = jnp.sum(jnp.where(mine, slot_table % position_count, 0), axis=1)
    down, up_query, up_keyval = select_adapters(
        index, (adapter_down_maps, adapter_up_query, adapter_up_key_value)
    )
    segment_row = token_request_ids[0]
    members = segment_row[:, None] == jnp.arange(STORE_REQUESTS, dtype=jnp.int32)[None, :]
    holder = jnp.sum(jnp.where(members, (my_slots // position_count)[None, :], 0), axis=1)
    mask = (holder[:, None] == jnp.arange(stores, dtype=jnp.int32)[None, :]).astype(jnp.float32)
    cosine, sine = rotary_tables(token_positions(segment_row))
    holds_keys = tensor_rank % 2 == 0
    key_cosine = jnp.where(holds_keys, cosine, 1.0)
    key_sine = jnp.where(holds_keys, sine, 0.0)

    rows, model_width = tokens.shape
    total = rows * n
    query_width = query_weight.shape[1]
    keyval_width = key_value_weight.shape[1]
    chunks = max(8, n)
    width = model_width // chunks
    pair_heads = keyval_width // HEAD_SIZE
    kv_used = max(query_width // HEAD_SIZE // (QUERY_HEADS // KEY_VALUE_HEADS), 1)
    two_ranks = 2 * ADAPTER_RANK
    hbm = pl.BlockSpec(memory_space=pl.ANY)
    vmem = pl.BlockSpec(memory_space=pltpu.VMEM)
    dma = pltpu.SemaphoreType.DMA
    query, own, other = pl.pallas_call(
        functools.partial(project_kernel, n, stores, chunks),
        in_specs=[hbm] * 6 + [vmem] * 5,
        out_specs=[vmem] * 3,
        out_shape=[
            jax.ShapeDtypeStruct((total, query_width), jnp.bfloat16),
            jax.ShapeDtypeStruct((kv_used, total, HEAD_SIZE), jnp.bfloat16),
            jax.ShapeDtypeStruct((kv_used, total, HEAD_SIZE), jnp.bfloat16),
        ],
        scratch_shapes=[
            pltpu.VMEM((chunks, total, width), jnp.bfloat16),
            pltpu.VMEM((model_width, query_width), jnp.bfloat16),
            pltpu.VMEM((model_width, keyval_width), jnp.bfloat16),
            pltpu.VMEM((total, query_width), jnp.float32),
            pltpu.VMEM((total, keyval_width), jnp.float32),
            pltpu.VMEM((stores, two_ranks, model_width // n), jnp.bfloat16),
            pltpu.VMEM((stores * ADAPTER_RANK, query_width), jnp.bfloat16),
            pltpu.VMEM((stores * ADAPTER_RANK, keyval_width), jnp.bfloat16),
            pltpu.VMEM((total, two_ranks), jnp.float32),
            pltpu.VMEM((n, rows, two_ranks), jnp.float32),
            pltpu.VMEM((total, two_ranks), jnp.bfloat16),
            pltpu.VMEM((pair_heads, total, HEAD_SIZE), jnp.bfloat16),
            pltpu.VMEM((kv_used, total, HEAD_SIZE), jnp.bfloat16),
            dma((chunks,)),
            dma((2, chunks)),
            dma((2, n, chunks)),
            dma((2, n, chunks)),
            dma((3, stores)),
            dma((3, stores)),
            dma((3,)),
            dma((n,)),
            dma((n,)),
            dma((n,)),
            dma((n,)),
            dma((2,)),
        ],
        compiler_params=pltpu.CompilerParams(
            collective_id=0, has_side_effects=True, vmem_limit_bytes=67043328
        ),
        name="project",
    )(
        tokens,
        query_weight,
        key_value_weight,
        down,
        up_query,
        up_keyval,
        mask,
        cosine,
        sine,
        key_cosine,
        key_sine,
    )
    keys = jnp.where(holds_keys, own, other)
    values = jnp.where(holds_keys, other, own)
    return attend(query, keys, values, segment_row)


def solution(mesh):
    return jax.shard_map(
        on_device,
        mesh=mesh,
        in_specs=(
            P(("groups", "store", "tensor"), None),
            P(None, "tensor"),
            P(None, "tensor"),
            P("store", None, "tensor"),
            P("store", None, "tensor"),
            P("store", None, "tensor"),
            P("groups"),
            P("groups", None),
            P(("groups", "store"), None),
        ),
        out_specs=P(("groups", "store"), "tensor"),
        check_vma=False,
    )
```

```python
import functools
import math

import jax
import jax.numpy as jnp
from jax import lax
from jax.experimental import pallas as pl
from jax.experimental.pallas import tpu as pltpu
from jax.sharding import PartitionSpec as P

MODEL_WIDTH = 8192
QUERY_HEADS = 64
KEY_VALUE_HEADS = 8
HEAD_SIZE = 128
ADAPTER_RANK = 64
STORE_REQUESTS = 4
TOK_ST = 512


adapter_scale = 2.0
rope_theta = 500000.0


MAX_RUN = 256
MESH = pl.DeviceIdType.MESH


def select_kernel(index_ref, down_ref, query_ref, keyval_ref, down_out, query_out, keyval_out):
    down_out[...] = down_ref[...]
    query_out[...] = query_ref[...]
    keyval_out[...] = keyval_ref[...]


def select_adapters(index, stacks):
    specs_in = [
        pl.BlockSpec((1,) + stack.shape[1:], lambda i, index_ref: (index_ref[i], 0, 0))
        for stack in stacks
    ]
    specs_out = [
        pl.BlockSpec((1,) + stack.shape[1:], lambda i, index_ref: (i, 0, 0)) for stack in stacks
    ]
    return pl.pallas_call(
        select_kernel,
        grid_spec=pltpu.PrefetchScalarGridSpec(
            num_scalar_prefetch=1,
            grid=(index.shape[0],),
            in_specs=specs_in,
            out_specs=specs_out,
        ),
        out_shape=[
            jax.ShapeDtypeStruct((index.shape[0],) + stack.shape[1:], stack.dtype)
            for stack in stacks
        ],
        name="select_adapters",
    )(index, *stacks)


def project_kernel(
    n,
    stores,
    chunks,
    position_count,
    tokens_ref,
    wq_hbm,
    wkv_hbm,
    down_hbm,
    upq_hbm,
    upkv_hbm,
    slot_ref,
    segment_ref,
    frequency_ref,
    out_ref,
    xbuf,
    wq,
    wkv,
    acc_q,
    acc_kv,
    down,
    upq,
    upkv,
    low_part,
    low_got,
    low_all,
    kv_heads,
    kv_got,
    keys_ref,
    values_ref,
    bias_ref,
    cos_ref,
    sin_ref,
    holder_ref,
    token_sem,
    weight_sem,
    recv_sem,
    send_sem,
    adapter_send,
    adapter_recv,
    adapter_own,
    part_send,
    part_recv,
    low_send,
    low_recv,
    kv_sem,
    out_sem,
):
    t = lax.axis_index("tensor")
    s = lax.axis_index("store")
    rows = tokens_ref.shape[0]
    width = tokens_ref.shape[1] // chunks
    total = rows * n
    query_width = wq.shape[1]
    keyval_width = wkv.shape[1]
    pair_heads = keyval_width // HEAD_SIZE
    head_local = query_width // HEAD_SIZE
    group_size = QUERY_HEADS // KEY_VALUE_HEADS
    kv_used = max(head_local // group_size, 1)

    def kv_first(rank):
        return rank * head_local // group_size - rank // 2 * pair_heads

    barrier = pltpu.get_barrier_semaphore()
    for d in range(1, n):
        pl.semaphore_signal(
            barrier, inc=1, device_id={"tensor": lax.rem(t + d, n)}, device_id_type=MESH
        )
    for d in range(1, stores):
        pl.semaphore_signal(
            barrier, inc=1, device_id={"store": lax.rem(s + d, stores)}, device_id_type=MESH
        )

    def own_copy(c):
        return pltpu.make_async_copy(
            tokens_ref.at[:, pl.ds(c * width, width)],
            xbuf.at[c, pl.ds(t * rows, rows), :],
            token_sem.at[c],
        )

    def weight_copies(c):
        part = pl.ds(c * width, width)
        return (
            pltpu.make_async_copy(wq_hbm.at[part, :], wq.at[part, :], weight_sem.at[0, c]),
            pltpu.make_async_copy(wkv_hbm.at[part, :], wkv.at[part, :], weight_sem.at[1, c]),
        )

    for c in range(chunks):
        own_copy(c).start()
        for copy in weight_copies(c):
            copy.start()
    adapter_pairs = ((down_hbm, down), (upq_hbm, upq), (upkv_hbm, upkv))

    def adapter_block(held, i, at):
        if i == 0:
            return held.at[at]
        return held.at[pl.ds(at * ADAPTER_RANK, ADAPTER_RANK), :]

    own_adapters = [
        pltpu.make_async_copy(source.at[s], adapter_block(held, i, s), adapter_own.at[i])
        for i, (source, held) in enumerate(adapter_pairs)
    ]
    for copy in own_adapters:
        copy.start()

    pl.semaphore_wait(barrier, n - 1 + stores - 1)

    def place(side, i):
        return chunks - 1 - i if side == 0 else i

    def stream_copy(side, p, i, own):
        c = place(side, i)
        shard = t - p if side == 0 else t + p
        held = xbuf.at[c, pl.ds(shard * rows, rows), :]
        source = tokens_ref.at[:, pl.ds(c * width, width)] if own else held
        return pltpu.make_async_remote_copy(
            src_ref=source,
            dst_ref=held,
            send_sem=send_sem.at[side, p, i],
            recv_sem=recv_sem.at[side, p, i],
            device_id={"tensor": t + 1 if side == 0 else t - 1},
            device_id_type=MESH,
        )

    def arrival(side, p, i):
        c = place(side, i)
        shard = t - p if side == 0 else t + p
        held = xbuf.at[c, pl.ds(shard * rows, rows), :]
        return pltpu.make_async_remote_copy(
            src_ref=held,
            dst_ref=held,
            send_sem=send_sem.at[side, p - 1, i],
            recv_sem=recv_sem.at[side, p - 1, i],
            device_id={"tensor": t - 1 if side == 0 else t + 1},
            device_id_type=MESH,
        )

    can_send = (t < n - 1, t > 0)
    for i in range(chunks):
        for side in range(2):

            @pl.when(can_send[side])
            def _():
                stream_copy(side, 0, i, True).start()

    adapter_sends = []
    for d in range(1, stores):
        for i, (source, held) in enumerate(adapter_pairs):
            peer = lax.rem(s + d, stores)
            copy = pltpu.make_async_remote_copy(
                src_ref=source.at[peer],
                dst_ref=adapter_block(held, i, s),
                send_sem=adapter_send.at[i, d],
                recv_sem=adapter_recv.at[i, d],
                device_id={"store": peer},
                device_id_type=MESH,
            )
            copy.start()
            adapter_sends.append(copy)

    tile_q = min(query_width, 512)

    def unit(c, shard, first):
        at = pl.ds(pl.multiple_of(shard * rows, rows), rows)
        part = pl.ds(pl.multiple_of(c * width, width), width)
        x = xbuf[c, at, :]
        add = jnp.dot(x, wkv[part, :], preferred_element_type=jnp.float32)
        if first:
            acc_kv[at, :] = add
        else:
            acc_kv[at, :] += add

        @pl.loop(0, query_width // tile_q)
        def _(k):
            columns = pl.ds(pl.multiple_of(k * tile_q, tile_q), tile_q)
            more = jnp.dot(
                xbuf[c, at, :], wq[part, columns], preferred_element_type=jnp.float32
            )
            if first:
                acc_q[at, columns] = more
            else:
                acc_q[at, columns] += more

    acc_q[...] = jnp.zeros_like(acc_q)
    acc_kv[...] = jnp.zeros_like(acc_kv)
    holds_keys = t % 2 == 0

    place_row = lax.broadcasted_iota(jnp.int32, (total, total), 0)
    place_column = lax.broadcasted_iota(jnp.int32, (total, total), 1)
    across = segment_ref[...].astype(jnp.float32)
    down_column = jnp.sum(jnp.where(place_row == place_column, across, 0.0), axis=1, keepdims=True)
    allowed = jnp.logical_and(down_column == across, place_row >= place_column)
    bias_ref[...] = jnp.where(allowed, 0.0, -1e30)
    first_index = jnp.sum(jnp.where(across < down_column, 1.0, 0.0), axis=1, keepdims=True)
    place_token = lax.broadcasted_iota(jnp.int32, (total, 1), 0).astype(jnp.float32)
    angles = (place_token - first_index) * frequency_ref[...]
    lane = lax.broadcasted_iota(jnp.int32, angles.shape, 1)
    sine = jnp.sin(angles)
    cos_ref[...] = jnp.cos(angles)
    sin_ref[...] = jnp.where(lane < HEAD_SIZE // 2, -sine, sine)
    holder = jnp.zeros((total, 1), jnp.float32)
    for k in range(STORE_REQUESTS):
        owner = lax.div(slot_ref[s, k], position_count).astype(jnp.float32)
        holder += jnp.where(down_column == float(k), owner, 0.0)
    holder_ref[...] = holder

    def mask_of(p):
        return jnp.where(holder_ref[...] == float(p), 1.0, 0.0)

    @pl.loop(0, chunks)
    def _(c):
        own_copy(c).wait()
        for copy in weight_copies(c):
            copy.wait()
        unit(c, t, False)

    for copy in own_adapters:
        copy.wait()

    share = chunks // n
    last_phase = jnp.maximum(t, n - 1 - t)
    low_at = share * (jnp.minimum(t, n - 1 - t) + 1) - 1

    def part_copy(d):
        to = lax.rem(t + d, n)
        return pltpu.make_async_remote_copy(
            src_ref=low_part.at[pl.ds(to * rows, rows), :],
            dst_ref=low_got.at[t],
            send_sem=part_send.at[d],
            recv_sem=part_recv.at[d],
            device_id={"tensor": to},
            device_id_type=MESH,
        )

    def part_arrival(d):
        source = lax.rem(t + n - d, n)
        return pltpu.make_async_remote_copy(
            src_ref=low_got.at[source],
            dst_ref=low_got.at[source],
            send_sem=part_send.at[d],
            recv_sem=part_recv.at[d],
            device_id={"tensor": source},
            device_id_type=MESH,
        )

    def low_copy(d):
        to = lax.rem(t + d, n)
        held = low_all.at[pl.ds(t * rows, rows), :]
        return pltpu.make_async_remote_copy(
            src_ref=held,
            dst_ref=held,
            send_sem=low_send.at[d],
            recv_sem=low_recv.at[d],
            device_id={"tensor": to},
            device_id_type=MESH,
        )

    def low_arrival(d):
        source = lax.rem(t + n - d, n)
        held = low_all.at[pl.ds(source * rows, rows), :]
        return pltpu.make_async_remote_copy(
            src_ref=held,
            dst_ref=held,
            send_sem=low_send.at[d],
            recv_sem=low_recv.at[d],
            device_id={"tensor": source},
            device_id_type=MESH,
        )

    def adapters_arrive():
        for d in range(1, stores):
            source = lax.rem(s + stores - d, stores)
            for i, (_, held) in enumerate(adapter_pairs):
                block = adapter_block(held, i, source)
                pltpu.make_async_remote_copy(
                    src_ref=block,
                    dst_ref=block,
                    send_sem=adapter_send.at[i, d],
                    recv_sem=adapter_recv.at[i, d],
                    device_id={"store": source},
                    device_id_type=MESH,
                ).wait_recv()

    def low_first():
        adapters_arrive()
        low_part[...] = jnp.zeros_like(low_part)
        for p in range(stores):
            picked = jnp.zeros(low_part.shape, jnp.float32)
            for k in range(share):
                picked += lax.dot_general(
                    xbuf[t * share + k],
                    down[p, :, k * width : (k + 1) * width],
                    (((1,), (1,)), ((), ())),
                    preferred_element_type=jnp.float32,
                )
            low_part[...] += picked * mask_of(p)
        for d in range(1, n):
            part_copy(d).start()

    def low_second():
        at = pl.ds(pl.multiple_of(t * rows, rows), rows)
        low_got[t] = low_part[at, :]
        for d in range(1, n):
            part_arrival(d).wait_recv()
        whole = low_got[0]
        for j in range(1, n):
            whole += low_got[j]
        low_all[at, :] = whole.astype(jnp.bfloat16)
        for d in range(1, n):
            low_copy(d).start()

    def low_third():
        for d in range(1, n):
            low_arrival(d).wait_recv()
        low = low_all[...].astype(jnp.float32)
        turned = pltpu.roll(low, ADAPTER_RANK, 1)
        in_lower = lax.broadcasted_iota(jnp.int32, low.shape, 1) < ADAPTER_RANK
        twice_q = jnp.where(in_lower, low, turned)
        twice_kv = jnp.where(in_lower, turned, low)
        masks = [
            jnp.where(in_lower, mask_of(2 * p), mask_of(2 * p + 1))
            for p in range(stores // 2)
        ]
        spread_q = jnp.concatenate([(twice_q * m).astype(jnp.bfloat16) for m in masks], axis=1)
        spread_kv = jnp.concatenate([(twice_kv * m).astype(jnp.bfloat16) for m in masks], axis=1)
        acc_kv[...] += adapter_scale * jnp.dot(
            spread_kv, upkv[...], preferred_element_type=jnp.float32
        )
        for k in range(query_width // tile_q):
            columns = slice(k * tile_q, (k + 1) * tile_q)
            acc_q[:, columns] += adapter_scale * jnp.dot(
                spread_q, upq[:, columns], preferred_element_type=jnp.float32
            )

    def rotated(value, cosine, sine):
        return value * cosine + pltpu.roll(value, HEAD_SIZE // 2, 1) * sine

    ends_first = t >= n - t
    early_start = pl.multiple_of(jnp.where(ends_first, rows, 0), rows)
    late_start = pl.multiple_of(jnp.where(ends_first, 0, total - rows), rows)
    partner = t + 1 - 2 * (t % 2)

    def finish_keyval(start, count):
        at = pl.ds(start, count)
        cosine = jnp.where(holds_keys, cos_ref[at, :], 1.0)
        sine = jnp.where(holds_keys, sin_ref[at, :], 0.0)
        for m in range(pair_heads):
            value = acc_kv[at, m * HEAD_SIZE : (m + 1) * HEAD_SIZE]
            kv_heads[m, at, :] = rotated(value, cosine, sine).astype(jnp.bfloat16)

    def keyval_copy(start, count, which):
        at = pl.ds(start, count)
        return pltpu.make_async_remote_copy(
            src_ref=kv_heads.at[pl.ds(kv_first(partner), kv_used), at, :],
            dst_ref=kv_got.at[:, at, :],
            send_sem=kv_sem.at[0, which],
            recv_sem=kv_sem.at[1, which],
            device_id={"tensor": partner},
            device_id_type=MESH,
        )

    depth = min(4, chunks)

    @pl.loop(0, (n - 1) * chunks)
    def _(step):
        p = step // chunks + 1
        i = step % chunks
        here = (t - p >= 0, t + p < n)
        for side in range(2):

            @pl.when(jnp.logical_and(here[side], can_send[side]))
            def _():
                back = step + chunks - depth
                arrival(side, p, i).wait_recv()
                stream_copy(side, back // chunks, back % chunks, False).wait_send()
                stream_copy(side, p, i, False).start()

            @pl.when(jnp.logical_and(here[side], jnp.logical_not(can_send[side])))
            def _():
                arrival(side, p, i).wait_recv()

        for side in range(2):

            @pl.when(here[side])
            def _():
                unit(place(side, i), t - p if side == 0 else t + p, False)

        @pl.when(jnp.logical_and(p == last_phase, i == low_at))
        def _():
            low_first()

        @pl.when(jnp.logical_and(p == last_phase, i == low_at + 1))
        def _():
            low_second()

        @pl.when(jnp.logical_and(p == last_phase, i == chunks - 2))
        def _():
            low_third()
            finish_keyval(early_start, total - rows)
            keyval_copy(early_start, total - rows, 0).start()

    finish_keyval(late_start, rows)
    keyval_copy(late_start, rows, 1).start()
    for copy in adapter_sends:
        copy.wait_send()
    for d in range(1, n):
        part_copy(d).wait_send()
        low_copy(d).wait_send()

    @pl.loop(0, chunks - depth)
    def _(k):
        for side in range(2):

            @pl.when(can_send[side])
            def _():
                stream_copy(side, 0, k, False).wait_send()

    @pl.loop(0, depth)
    def _(k):
        for side in range(2):

            @pl.when(can_send[side])
            def _():
                reach = t if side == 0 else n - 1 - t
                back = (reach + 1) * chunks - depth + k
                stream_copy(side, back // chunks, back % chunks, False).wait_send()

    per_chunk = width // HEAD_SIZE
    for h in range(head_local):
        columns = slice(h * HEAD_SIZE, (h + 1) * HEAD_SIZE)
        inside = h % per_chunk * HEAD_SIZE
        xbuf[h // per_chunk, :, inside : inside + HEAD_SIZE] = rotated(
            acc_q[:, columns], cos_ref[...], sin_ref[...]
        ).astype(jnp.bfloat16)

    keyval_copy(early_start, total - rows, 0).wait()
    keyval_copy(late_start, rows, 1).wait()
    own_first = kv_first(t)
    for g in range(kv_used):
        values_ref[g, :, HEAD_SIZE:] = jnp.ones((total, HEAD_SIZE), jnp.bfloat16)

        @pl.when(holds_keys)
        def _():
            keys_ref[g] = kv_heads[own_first + g]
            values_ref[g, :, :HEAD_SIZE] = kv_got[g]

        @pl.when(jnp.logical_not(holds_keys))
        def _():
            keys_ref[g] = kv_got[g]
            values_ref[g, :, :HEAD_SIZE] = kv_heads[own_first + g]

    per_kv = head_local // kv_used
    batch = 4
    batches_per_chunk = per_chunk // batch
    block = 128
    scale = 1.0 / math.sqrt(HEAD_SIZE) / math.log(2.0)

    def out_copy(q):
        inside = pl.multiple_of(q % batches_per_chunk * batch * HEAD_SIZE, batch * HEAD_SIZE)
        whole = pl.multiple_of(q * batch * HEAD_SIZE, batch * HEAD_SIZE)
        return pltpu.make_async_copy(
            xbuf.at[q // batches_per_chunk, :, pl.ds(inside, batch * HEAD_SIZE)],
            out_ref.at[:, pl.ds(whole, batch * HEAD_SIZE)],
            out_sem.at[q],
        )

    @pl.loop(0, head_local // batch)
    def _(q):
        chunk = q // batches_per_chunk
        base = q % batches_per_chunk * batch
        g = q * batch // per_kv
        for pair in range(batch // 2):
            lanes = [
                pl.ds(pl.multiple_of((base + 2 * pair + k) * HEAD_SIZE, HEAD_SIZE), HEAD_SIZE)
                for k in range(2)
            ]
            for b in range(total // block):
                low = max(0, b * block - MAX_RUN)
                high = (b + 1) * block
                at = slice(b * block, high)
                stacked = jnp.concatenate([xbuf[chunk, at, ln] for ln in lanes], axis=0)
                scores = lax.dot_general(
                    stacked,
                    keys_ref[g, low:high, :],
                    (((1,), (1,)), ((), ())),
                    preferred_element_type=jnp.float32,
                )
                scores = scores.reshape(2, block, high - low) + bias_ref[at, low:high][None]
                scores = (scores - jnp.max(scores, axis=2, keepdims=True)) * scale
                weights = jnp.exp2(scores).astype(jnp.bfloat16).reshape(2 * block, high - low)
                mixed = jnp.dot(
                    weights, values_ref[g, low:high, :], preferred_element_type=jnp.float32
                )
                mixed = (mixed[:, :HEAD_SIZE] / mixed[:, HEAD_SIZE:]).astype(jnp.bfloat16)
                for k in range(2):
                    xbuf[chunk, at, lanes[k]] = mixed[k * block : (k + 1) * block]
        out_copy(q).start()

    @pl.loop(0, head_local // batch)
    def _(q):
        out_copy(q).wait()


def on_device(
    tokens,
    query_weight,
    key_value_weight,
    adapter_down_maps,
    adapter_up_query,
    adapter_up_key_value,
    adapter_row_table,
    request_adapter_ids,
    token_request_ids,
):
    store_rank = lax.axis_index("store")
    n = lax.axis_size("tensor")
    stores = lax.axis_size("store")
    position_count = adapter_down_maps.shape[0]
    adapter_total = adapter_row_table.shape[0]
    lookup = (
        request_adapter_ids[:, :, None] == jnp.arange(adapter_total, dtype=jnp.int32)[None, None, :]
    ).astype(jnp.int32)
    slot_table = jnp.sum(lookup * adapter_row_table[None, None, :], axis=2)
    mine = slot_table // position_count == store_rank
    index = jnp.sum(jnp.where(mine, slot_table % position_count, 0), axis=1)
    down, up_query, up_keyval = select_adapters(
        index, (adapter_down_maps, adapter_up_query, adapter_up_key_value)
    )
    half_size = HEAD_SIZE // 2
    exponent = jnp.arange(half_size, dtype=jnp.float32) * (2.0 / HEAD_SIZE)
    frequency = jnp.exp(-exponent * math.log(rope_theta))
    frequency = jnp.concatenate([frequency, frequency])[None, :]

    rows, model_width = tokens.shape
    total = rows * n
    query_width = query_weight.shape[1]
    keyval_width = key_value_weight.shape[1]
    chunks = max(8, n)
    width = model_width // chunks
    pair_heads = keyval_width // HEAD_SIZE
    kv_used = max(query_width // HEAD_SIZE // (QUERY_HEADS // KEY_VALUE_HEADS), 1)
    two_ranks = 2 * ADAPTER_RANK
    hbm = pl.BlockSpec(memory_space=pl.ANY)
    vmem = pl.BlockSpec(memory_space=pltpu.VMEM)
    dma = pltpu.SemaphoreType.DMA
    return pl.pallas_call(
        functools.partial(project_kernel, n, stores, chunks, position_count),
        in_specs=[hbm] * 6 + [pl.BlockSpec(memory_space=pltpu.SMEM), vmem, vmem],
        out_specs=hbm,
        out_shape=jax.ShapeDtypeStruct((total, query_width), jnp.bfloat16),
        scratch_shapes=[
            pltpu.VMEM((chunks, total, width), jnp.bfloat16),
            pltpu.VMEM((model_width, query_width), jnp.bfloat16),
            pltpu.VMEM((model_width, keyval_width), jnp.bfloat16),
            pltpu.VMEM((total, query_width), jnp.float32),
            pltpu.VMEM((total, keyval_width), jnp.float32),
            pltpu.VMEM((stores, two_ranks, model_width // n), jnp.bfloat16),
            pltpu.VMEM((stores * ADAPTER_RANK, query_width), jnp.bfloat16),
            pltpu.VMEM((stores * ADAPTER_RANK, keyval_width), jnp.bfloat16),
            pltpu.VMEM((total, two_ranks), jnp.float32),
            pltpu.VMEM((n, rows, two_ranks), jnp.float32),
            pltpu.VMEM((total, two_ranks), jnp.bfloat16),
            pltpu.VMEM((pair_heads, total, HEAD_SIZE), jnp.bfloat16),
            pltpu.VMEM((kv_used, total, HEAD_SIZE), jnp.bfloat16),
            pltpu.VMEM((kv_used, total, HEAD_SIZE), jnp.bfloat16),
            pltpu.VMEM((kv_used, total, 2 * HEAD_SIZE), jnp.bfloat16),
            pltpu.VMEM((total, total), jnp.float32),
            pltpu.VMEM((total, HEAD_SIZE), jnp.float32),
            pltpu.VMEM((total, HEAD_SIZE), jnp.float32),
            pltpu.VMEM((total, 1), jnp.float32),
            dma((chunks,)),
            dma((2, chunks)),
            dma((2, n, chunks)),
            dma((2, n, chunks)),
            dma((3, stores)),
            dma((3, stores)),
            dma((3,)),
            dma((n,)),
            dma((n,)),
            dma((n,)),
            dma((n,)),
            dma((2, 2)),
            dma((query_width // HEAD_SIZE // 4,)),
        ],
        compiler_params=pltpu.CompilerParams(
            collective_id=0, has_side_effects=True, vmem_limit_bytes=67043328
        ),
        name="project",
    )(
        tokens,
        query_weight,
        key_value_weight,
        down,
        up_query,
        up_keyval,
        slot_table,
        token_request_ids,
        frequency,
    )


def solution(mesh):
    return jax.shard_map(
        on_device,
        mesh=mesh,
        in_specs=(
            P(("groups", "store", "tensor"), None),
            P(None, "tensor"),
            P(None, "tensor"),
            P("store", None, "tensor"),
            P("store", None, "tensor"),
            P("store", None, "tensor"),
            P("groups"),
            P("groups", None),
            P(("groups", "store"), None),
        ),
        out_specs=P(("groups", "store"), "tensor"),
        check_vma=False,
    )
```

```python
import functools
import math

import jax
import jax.numpy as jnp
from jax import lax
from jax.experimental import pallas as pl
from jax.experimental.pallas import tpu as pltpu
from jax.sharding import PartitionSpec as P

MODEL_WIDTH = 8192
QUERY_HEADS = 64
KEY_VALUE_HEADS = 8
HEAD_SIZE = 128
ADAPTER_RANK = 64
STORE_REQUESTS = 4
TOK_ST = 512


adapter_scale = 2.0
rope_theta = 500000.0


MAX_RUN = 256
MESH = pl.DeviceIdType.MESH


def select_kernel(
    position_count, table_ref, request_ref, down_hbm, query_hbm, keyval_hbm, *rest
):
    outs, held, in_sem, out_sem = rest[:3], rest[3:6], rest[6], rest[7]
    s = lax.axis_index("store")
    stacks = (down_hbm, query_hbm, keyval_hbm)
    loads = []
    for i in range(request_ref.shape[0]):
        index = 0
        for k in range(STORE_REQUESTS):
            slot = table_ref[request_ref[i, k]]
            index += jnp.where(
                lax.div(slot, position_count) == s, lax.rem(slot, position_count), 0
            )
        for j in range(3):
            copy = pltpu.make_async_copy(stacks[j].at[index], held[j].at[i], in_sem.at[j, i])
            copy.start()
            loads.append((j, i, copy))
    stores = []
    for j, i, copy in loads:
        copy.wait()
        store = pltpu.make_async_copy(held[j].at[i], outs[j].at[i], out_sem.at[j, i])
        store.start()
        stores.append(store)
    for store in stores:
        store.wait()


def select_adapters(table, requests, stacks):
    hbm = pl.BlockSpec(memory_space=pl.ANY)
    smem = pl.BlockSpec(memory_space=pltpu.SMEM)
    count = requests.shape[0]
    shapes = [(count,) + stack.shape[1:] for stack in stacks]
    return pl.pallas_call(
        functools.partial(select_kernel, stacks[0].shape[0]),
        in_specs=[smem, smem] + [hbm] * 3,
        out_specs=[hbm] * 3,
        out_shape=[jax.ShapeDtypeStruct(shape, jnp.bfloat16) for shape in shapes],
        scratch_shapes=[pltpu.VMEM(shape, jnp.bfloat16) for shape in shapes]
        + [pltpu.SemaphoreType.DMA((3, count)), pltpu.SemaphoreType.DMA((3, count))],
        name="select_adapters",
    )(table, requests, *stacks)


def project_kernel(
    n,
    stores,
    chunks,
    position_count,
    tokens_ref,
    wq_hbm,
    wkv_hbm,
    down_hbm,
    upq_hbm,
    upkv_hbm,
    table_ref,
    request_ref,
    segment_ref,
    out_ref,
    xbuf,
    wq,
    wkv,
    acc_q,
    acc_kv,
    down,
    upq,
    upkv,
    low_part,
    low_own,
    low_got,
    low_all,
    kv_heads,
    kv_got,
    keys_ref,
    values_ref,
    bias_ref,
    cos_ref,
    sin_ref,
    holder_ref,
    token_sem,
    weight_sem,
    recv_sem,
    send_sem,
    adapter_send,
    adapter_recv,
    adapter_own,
    part_send,
    part_recv,
    low_send,
    low_recv,
    kv_sem,
    out_sem,
):
    t = lax.axis_index("tensor")
    s = lax.axis_index("store")
    rows = tokens_ref.shape[0]
    width = tokens_ref.shape[1] // chunks
    total = rows * n
    query_width = wq.shape[1]
    keyval_width = wkv.shape[1]
    pair_heads = keyval_width // HEAD_SIZE
    head_local = query_width // HEAD_SIZE
    group_size = QUERY_HEADS // KEY_VALUE_HEADS
    kv_used = max(head_local // group_size, 1)

    def kv_first(rank):
        return rank * head_local // group_size - rank // 2 * pair_heads

    barrier = pltpu.get_barrier_semaphore()
    for d in range(1, n):
        pl.semaphore_signal(
            barrier, inc=1, device_id={"tensor": lax.rem(t + d, n)}, device_id_type=MESH
        )
    for d in range(1, stores):
        pl.semaphore_signal(
            barrier, inc=1, device_id={"store": lax.rem(s + d, stores)}, device_id_type=MESH
        )

    def own_copy(c):
        return pltpu.make_async_copy(
            tokens_ref.at[:, pl.ds(c * width, width)],
            xbuf.at[c, pl.ds(t * rows, rows), :],
            token_sem.at[c],
        )

    def weight_copies(c):
        part = pl.ds(c * width, width)
        return (
            pltpu.make_async_copy(wq_hbm.at[part, :], wq.at[part, :], weight_sem.at[0, c]),
            pltpu.make_async_copy(wkv_hbm.at[part, :], wkv.at[part, :], weight_sem.at[1, c]),
        )

    for c in range(chunks):
        own_copy(c).start()
        for copy in weight_copies(c):
            copy.start()
    adapter_pairs = ((down_hbm, down), (upq_hbm, upq), (upkv_hbm, upkv))

    def adapter_block(held, i, at):
        if i == 0:
            return held.at[at]
        return held.at[pl.ds(at * ADAPTER_RANK, ADAPTER_RANK), :]

    own_adapters = [
        pltpu.make_async_copy(source.at[s], adapter_block(held, i, s), adapter_own.at[i])
        for i, (source, held) in enumerate(adapter_pairs)
    ]
    for copy in own_adapters:
        copy.start()

    pl.semaphore_wait(barrier, n - 1 + stores - 1)

    def place(side, i):
        return chunks - 1 - i if side == 0 else i

    def stream_copy(side, p, i, own):
        c = place(side, i)
        shard = t - p if side == 0 else t + p
        held = xbuf.at[c, pl.ds(shard * rows, rows), :]
        source = tokens_ref.at[:, pl.ds(c * width, width)] if own else held
        return pltpu.make_async_remote_copy(
            src_ref=source,
            dst_ref=held,
            send_sem=send_sem.at[side, p, i],
            recv_sem=recv_sem.at[side, p, i],
            device_id={"tensor": t + 1 if side == 0 else t - 1},
            device_id_type=MESH,
        )

    def arrival(side, p, i):
        c = place(side, i)
        shard = t - p if side == 0 else t + p
        held = xbuf.at[c, pl.ds(shard * rows, rows), :]
        return pltpu.make_async_remote_copy(
            src_ref=held,
            dst_ref=held,
            send_sem=send_sem.at[side, p - 1, i],
            recv_sem=recv_sem.at[side, p - 1, i],
            device_id={"tensor": t - 1 if side == 0 else t + 1},
            device_id_type=MESH,
        )

    can_send = (t < n - 1, t > 0)
    for i in range(chunks):
        for side in range(2):

            @pl.when(can_send[side])
            def _():
                stream_copy(side, 0, i, True).start()

    adapter_sends = []
    for d in range(1, stores):
        for i, (source, held) in enumerate(adapter_pairs):
            peer = lax.rem(s + d, stores)
            copy = pltpu.make_async_remote_copy(
                src_ref=source.at[peer],
                dst_ref=adapter_block(held, i, s),
                send_sem=adapter_send.at[i, d],
                recv_sem=adapter_recv.at[i, d],
                device_id={"store": peer},
                device_id_type=MESH,
            )
            copy.start()
            adapter_sends.append(copy)

    tile_q = min(query_width, 512)

    def unit(c, shard, first):
        at = pl.ds(pl.multiple_of(shard * rows, rows), rows)
        part = pl.ds(pl.multiple_of(c * width, width), width)
        x = xbuf[c, at, :]
        add = jnp.dot(x, wkv[part, :], preferred_element_type=jnp.float32)
        if first:
            acc_kv[at, :] = add
        else:
            acc_kv[at, :] += add

        @pl.loop(0, query_width // tile_q)
        def _(k):
            columns = pl.ds(pl.multiple_of(k * tile_q, tile_q), tile_q)
            more = jnp.dot(
                xbuf[c, at, :], wq[part, columns], preferred_element_type=jnp.float32
            )
            if first:
                acc_q[at, columns] = more
            else:
                acc_q[at, columns] += more

    acc_q[...] = jnp.zeros_like(acc_q)
    acc_kv[...] = jnp.zeros_like(acc_kv)
    holds_keys = t % 2 == 0

    place_row = lax.broadcasted_iota(jnp.int32, (total, total), 0)
    place_column = lax.broadcasted_iota(jnp.int32, (total, total), 1)
    across = segment_ref[...].astype(jnp.float32)
    down_column = jnp.sum(jnp.where(place_row == place_column, across, 0.0), axis=1, keepdims=True)
    allowed = jnp.logical_and(down_column == across, place_row >= place_column)
    bias_ref[...] = jnp.where(allowed, 0.0, -1e30)
    first_index = jnp.sum(jnp.where(across < down_column, 1.0, 0.0), axis=1, keepdims=True)
    place_token = lax.broadcasted_iota(jnp.int32, (total, 1), 0).astype(jnp.float32)
    lane = lax.broadcasted_iota(jnp.int32, (total, HEAD_SIZE), 1)
    exponent = lax.rem(lane, HEAD_SIZE // 2).astype(jnp.float32) * (2.0 / HEAD_SIZE)
    angles = (place_token - first_index) * jnp.exp(-exponent * math.log(rope_theta))
    sine = jnp.sin(angles)
    cos_ref[...] = jnp.cos(angles)
    sin_ref[...] = jnp.where(lane < HEAD_SIZE // 2, -sine, sine)
    holder = jnp.zeros((total, 1), jnp.float32)
    for k in range(STORE_REQUESTS):
        owner = lax.div(table_ref[request_ref[s, k]], position_count).astype(jnp.float32)
        holder += jnp.where(down_column == float(k), owner, 0.0)
    holder_ref[...] = holder

    def mask_of(p):
        return jnp.where(holder_ref[...] == float(p), 1.0, 0.0)

    @pl.loop(0, chunks)
    def _(c):
        own_copy(c).wait()
        for copy in weight_copies(c):
            copy.wait()
        unit(c, t, False)

    for copy in own_adapters:
        copy.wait()

    share = chunks // n
    last_phase = jnp.maximum(t, n - 1 - t)
    low_at = share * (jnp.minimum(t, n - 1 - t) + 1) - 1

    def part_copy(d):
        to = lax.rem(t + d, n)
        return pltpu.make_async_remote_copy(
            src_ref=low_part.at[pl.ds(to * rows, rows), :],
            dst_ref=low_got.at[t],
            send_sem=part_send.at[d],
            recv_sem=part_recv.at[d],
            device_id={"tensor": to},
            device_id_type=MESH,
        )

    def part_arrival(d):
        source = lax.rem(t + n - d, n)
        return pltpu.make_async_remote_copy(
            src_ref=low_got.at[source],
            dst_ref=low_got.at[source],
            send_sem=part_send.at[d],
            recv_sem=part_recv.at[d],
            device_id={"tensor": source},
            device_id_type=MESH,
        )

    def low_copy(d):
        to = lax.rem(t + d, n)
        held = low_all.at[pl.ds(t * rows, rows), :]
        return pltpu.make_async_remote_copy(
            src_ref=held,
            dst_ref=held,
            send_sem=low_send.at[d],
            recv_sem=low_recv.at[d],
            device_id={"tensor": to},
            device_id_type=MESH,
        )

    def low_arrival(d):
        source = lax.rem(t + n - d, n)
        held = low_all.at[pl.ds(source * rows, rows), :]
        return pltpu.make_async_remote_copy(
            src_ref=held,
            dst_ref=held,
            send_sem=low_send.at[d],
            recv_sem=low_recv.at[d],
            device_id={"tensor": source},
            device_id_type=MESH,
        )

    def adapters_arrive():
        for d in range(1, stores):
            source = lax.rem(s + stores - d, stores)
            for i, (_, held) in enumerate(adapter_pairs):
                block = adapter_block(held, i, source)
                pltpu.make_async_remote_copy(
                    src_ref=block,
                    dst_ref=block,
                    send_sem=adapter_send.at[i, d],
                    recv_sem=adapter_recv.at[i, d],
                    device_id={"store": source},
                    device_id_type=MESH,
                ).wait_recv()

    def low_first():
        adapters_arrive()
        summed = jnp.zeros(low_part.shape, jnp.float32)
        for p in range(stores):
            picked = jnp.zeros(low_part.shape, jnp.float32)
            for k in range(share):
                picked += lax.dot_general(
                    xbuf[t * share + k],
                    down[p, :, k * width : (k + 1) * width],
                    (((1,), (1,)), ((), ())),
                    preferred_element_type=jnp.float32,
                )
            summed += picked * mask_of(p)
        low_part[...] = summed.astype(jnp.bfloat16)
        low_own[...] = summed
        for d in range(1, n):
            part_copy(d).start()

    def low_second():
        at = pl.ds(pl.multiple_of(t * rows, rows), rows)
        whole = low_own[at, :]
        for d in range(1, n):
            part_arrival(d).wait_recv()
            whole += low_got[lax.rem(t + n - d, n)].astype(jnp.float32)
        low_all[at, :] = whole.astype(jnp.bfloat16)
        for d in range(1, n):
            low_copy(d).start()

    def low_third():
        for d in range(1, n):
            low_arrival(d).wait_recv()
        low = low_all[...].astype(jnp.float32)
        turned = pltpu.roll(low, ADAPTER_RANK, 1)
        in_lower = lax.broadcasted_iota(jnp.int32, low.shape, 1) < ADAPTER_RANK
        twice_q = jnp.where(in_lower, low, turned)
        twice_kv = jnp.where(in_lower, turned, low)
        masks = [
            jnp.where(in_lower, mask_of(2 * p), mask_of(2 * p + 1))
            for p in range(stores // 2)
        ]
        spread_q = jnp.concatenate([(twice_q * m).astype(jnp.bfloat16) for m in masks], axis=1)
        spread_kv = jnp.concatenate([(twice_kv * m).astype(jnp.bfloat16) for m in masks], axis=1)
        acc_kv[...] += adapter_scale * jnp.dot(
            spread_kv, upkv[...], preferred_element_type=jnp.float32
        )
        for k in range(query_width // tile_q):
            columns = slice(k * tile_q, (k + 1) * tile_q)
            acc_q[:, columns] += adapter_scale * jnp.dot(
                spread_q, upq[:, columns], preferred_element_type=jnp.float32
            )

    def rotated(value, cosine, sine):
        return value * cosine + pltpu.roll(value, HEAD_SIZE // 2, 1) * sine

    ends_first = t >= n - t
    early_start = pl.multiple_of(jnp.where(ends_first, rows, 0), rows)
    late_start = pl.multiple_of(jnp.where(ends_first, 0, total - rows), rows)
    partner = t + 1 - 2 * (t % 2)

    def finish_keyval(start, count):
        at = pl.ds(start, count)
        cosine = jnp.where(holds_keys, cos_ref[at, :], 1.0)
        sine = jnp.where(holds_keys, sin_ref[at, :], 0.0)
        for m in range(pair_heads):
            value = acc_kv[at, m * HEAD_SIZE : (m + 1) * HEAD_SIZE]
            kv_heads[m, at, :] = rotated(value, cosine, sine).astype(jnp.bfloat16)

    def keyval_copy(start, count, which):
        at = pl.ds(start, count)
        return pltpu.make_async_remote_copy(
            src_ref=kv_heads.at[pl.ds(kv_first(partner), kv_used), at, :],
            dst_ref=kv_got.at[:, at, :],
            send_sem=kv_sem.at[0, which],
            recv_sem=kv_sem.at[1, which],
            device_id={"tensor": partner},
            device_id_type=MESH,
        )

    depth = min(4, chunks)

    @pl.loop(0, (n - 1) * chunks)
    def _(step):
        p = step // chunks + 1
        i = step % chunks
        here = (t - p >= 0, t + p < n)
        for side in range(2):

            @pl.when(jnp.logical_and(here[side], can_send[side]))
            def _():
                back = step + chunks - depth
                arrival(side, p, i).wait_recv()
                stream_copy(side, back // chunks, back % chunks, False).wait_send()
                stream_copy(side, p, i, False).start()

            @pl.when(jnp.logical_and(here[side], jnp.logical_not(can_send[side])))
            def _():
                arrival(side, p, i).wait_recv()

        for side in range(2):

            @pl.when(here[side])
            def _():
                unit(place(side, i), t - p if side == 0 else t + p, False)

        @pl.when(jnp.logical_and(p == last_phase, i == low_at))
        def _():
            low_first()

        @pl.when(jnp.logical_and(p == last_phase, i == low_at + 1))
        def _():
            low_second()

        @pl.when(jnp.logical_and(p == last_phase, i == chunks - 2))
        def _():
            low_third()
            finish_keyval(early_start, total - rows)
            keyval_copy(early_start, total - rows, 0).start()

    finish_keyval(late_start, rows)
    keyval_copy(late_start, rows, 1).start()
    for copy in adapter_sends:
        copy.wait_send()
    for d in range(1, n):
        part_copy(d).wait_send()
        low_copy(d).wait_send()

    @pl.loop(0, chunks - depth)
    def _(k):
        for side in range(2):

            @pl.when(can_send[side])
            def _():
                stream_copy(side, 0, k, False).wait_send()

    @pl.loop(0, depth)
    def _(k):
        for side in range(2):

            @pl.when(can_send[side])
            def _():
                reach = t if side == 0 else n - 1 - t
                back = (reach + 1) * chunks - depth + k
                stream_copy(side, back // chunks, back % chunks, False).wait_send()

    per_chunk = width // HEAD_SIZE
    for h in range(head_local):
        columns = slice(h * HEAD_SIZE, (h + 1) * HEAD_SIZE)
        inside = h % per_chunk * HEAD_SIZE
        xbuf[h // per_chunk, :, inside : inside + HEAD_SIZE] = rotated(
            acc_q[:, columns], cos_ref[...], sin_ref[...]
        ).astype(jnp.bfloat16)

    keyval_copy(early_start, total - rows, 0).wait()
    keyval_copy(late_start, rows, 1).wait()
    own_first = kv_first(t)
    for g in range(kv_used):
        values_ref[g, :, HEAD_SIZE:] = jnp.ones((total, HEAD_SIZE), jnp.bfloat16)

        @pl.when(holds_keys)
        def _():
            keys_ref[g] = kv_heads[own_first + g]
            values_ref[g, :, :HEAD_SIZE] = kv_got[g]

        @pl.when(jnp.logical_not(holds_keys))
        def _():
            keys_ref[g] = kv_got[g]
            values_ref[g, :, :HEAD_SIZE] = kv_heads[own_first + g]

    per_kv = head_local // kv_used
    batch = min(8, per_kv, per_chunk)
    batches_per_chunk = per_chunk // batch
    block = 128
    scale = 1.0 / math.sqrt(HEAD_SIZE) / math.log(2.0)

    def out_copy(q):
        whole = pl.multiple_of(q * batch * HEAD_SIZE, batch * HEAD_SIZE)
        return pltpu.make_async_copy(
            wq.at[pl.ds(0, total), pl.ds(whole, batch * HEAD_SIZE)],
            out_ref.at[:, pl.ds(whole, batch * HEAD_SIZE)],
            out_sem.at[q],
        )

    @pl.loop(0, head_local // batch)
    def _(q):
        chunk = q // batches_per_chunk
        base = q % batches_per_chunk * batch
        g = q * batch // per_kv
        for pair in range(batch // 2):
            lanes = [
                pl.ds(pl.multiple_of((base + 2 * pair + k) * HEAD_SIZE, HEAD_SIZE), HEAD_SIZE)
                for k in range(2)
            ]
            out_lanes = [
                pl.ds(
                    pl.multiple_of((q * batch + 2 * pair + k) * HEAD_SIZE, HEAD_SIZE), HEAD_SIZE
                )
                for k in range(2)
            ]
            for b in range(total // block):
                low = max(0, b * block - MAX_RUN)
                high = (b + 1) * block
                at = slice(b * block, high)
                stacked = jnp.concatenate([xbuf[chunk, at, ln] for ln in lanes], axis=0)
                scores = lax.dot_general(
                    stacked,
                    keys_ref[g, low:high, :],
                    (((1,), (1,)), ((), ())),
                    preferred_element_type=jnp.float32,
                )
                scores = scores.reshape(2, block, high - low) + bias_ref[at, low:high][None]
                scores = (scores - jnp.max(scores, axis=2, keepdims=True)) * scale
                weights = jnp.exp2(scores).astype(jnp.bfloat16).reshape(2 * block, high - low)
                mixed = jnp.dot(
                    weights, values_ref[g, low:high, :], preferred_element_type=jnp.float32
                )
                mixed = (mixed[:, :HEAD_SIZE] / mixed[:, HEAD_SIZE:]).astype(jnp.bfloat16)
                for k in range(2):
                    wq[at, out_lanes[k]] = mixed[k * block : (k + 1) * block]
        out_copy(q).start()

    @pl.loop(0, head_local // batch)
    def _(q):
        out_copy(q).wait()


def on_device(
    tokens,
    query_weight,
    key_value_weight,
    adapter_down_maps,
    adapter_up_query,
    adapter_up_key_value,
    adapter_row_table,
    request_adapter_ids,
    token_request_ids,
):
    n = lax.axis_size("tensor")
    stores = lax.axis_size("store")
    position_count = adapter_down_maps.shape[0]
    down, up_query, up_keyval = select_adapters(
        adapter_row_table,
        request_adapter_ids,
        (adapter_down_maps, adapter_up_query, adapter_up_key_value),
    )
    rows, model_width = tokens.shape
    total = rows * n
    query_width = query_weight.shape[1]
    keyval_width = key_value_weight.shape[1]
    chunks = max(8, n)
    width = model_width // chunks
    pair_heads = keyval_width // HEAD_SIZE
    kv_used = max(query_width // HEAD_SIZE // (QUERY_HEADS // KEY_VALUE_HEADS), 1)
    two_ranks = 2 * ADAPTER_RANK
    hbm = pl.BlockSpec(memory_space=pl.ANY)
    vmem = pl.BlockSpec(memory_space=pltpu.VMEM)
    smem = pl.BlockSpec(memory_space=pltpu.SMEM)
    dma = pltpu.SemaphoreType.DMA
    return pl.pallas_call(
        functools.partial(project_kernel, n, stores, chunks, position_count),
        in_specs=[hbm] * 6 + [smem, smem, vmem],
        out_specs=hbm,
        out_shape=jax.ShapeDtypeStruct((total, query_width), jnp.bfloat16),
        scratch_shapes=[
            pltpu.VMEM((chunks, total, width), jnp.bfloat16),
            pltpu.VMEM((model_width, query_width), jnp.bfloat16),
            pltpu.VMEM((model_width, keyval_width), jnp.bfloat16),
            pltpu.VMEM((total, query_width), jnp.float32),
            pltpu.VMEM((total, keyval_width), jnp.float32),
            pltpu.VMEM((stores, two_ranks, model_width // n), jnp.bfloat16),
            pltpu.VMEM((stores * ADAPTER_RANK, query_width), jnp.bfloat16),
            pltpu.VMEM((stores * ADAPTER_RANK, keyval_width), jnp.bfloat16),
            pltpu.VMEM((total, two_ranks), jnp.bfloat16),
            pltpu.VMEM((total, two_ranks), jnp.float32),
            pltpu.VMEM((n, rows, two_ranks), jnp.bfloat16),
            pltpu.VMEM((total, two_ranks), jnp.bfloat16),
            pltpu.VMEM((pair_heads, total, HEAD_SIZE), jnp.bfloat16),
            pltpu.VMEM((kv_used, total, HEAD_SIZE), jnp.bfloat16),
            pltpu.VMEM((kv_used, total, HEAD_SIZE), jnp.bfloat16),
            pltpu.VMEM((kv_used, total, 2 * HEAD_SIZE), jnp.bfloat16),
            pltpu.VMEM((total, total), jnp.float32),
            pltpu.VMEM((total, HEAD_SIZE), jnp.float32),
            pltpu.VMEM((total, HEAD_SIZE), jnp.float32),
            pltpu.VMEM((total, 1), jnp.float32),
            dma((chunks,)),
            dma((2, chunks)),
            dma((2, n, chunks)),
            dma((2, n, chunks)),
            dma((3, stores)),
            dma((3, stores)),
            dma((3,)),
            dma((n,)),
            dma((n,)),
            dma((n,)),
            dma((n,)),
            dma((2, 2)),
            dma((query_width // HEAD_SIZE // 4,)),
        ],
        compiler_params=pltpu.CompilerParams(
            collective_id=0, has_side_effects=True, vmem_limit_bytes=67043328
        ),
        name="project",
    )(
        tokens,
        query_weight,
        key_value_weight,
        down,
        up_query,
        up_keyval,
        adapter_row_table,
        request_adapter_ids,
        token_request_ids,
    )


def solution(mesh):
    return jax.shard_map(
        on_device,
        mesh=mesh,
        in_specs=(
            P(("groups", "store", "tensor"), None),
            P(None, "tensor"),
            P(None, "tensor"),
            P("store", None, "tensor"),
            P("store", None, "tensor"),
            P("store", None, "tensor"),
            P("groups"),
            P("groups", None),
            P(("groups", "store"), None),
        ),
        out_specs=P(("groups", "store"), "tensor"),
        check_vma=False,
    )
```
